32 devices in a mesh: groups: 2 (over y), seq: 16 (over z, x, core).
Axes of the slice: x: 2, y: 2, z: 4, core: 2. Of those that a mesh axis runs over, the one named last changes fastest.
Arguments:
- queries: bfloat16 [8192, 2048], P(('groups', 'seq')), parts along dimension 0, may hold values from -60 to 60
- keys: bfloat16 [8192, 1024], P(('groups', 'seq')), parts along dimension 0, may hold values from -6 to 6
- values: bfloat16 [8192, 1024], P(('groups', 'seq')), parts along dimension 0, may hold values from -6 to 6
- residual: bfloat16 [8192, 2688], P(('groups', 'seq')), parts along dimension 0, may hold values from -6 to 6
- out_weight: bfloat16 [2048, 2688], P('seq'), may hold values from -2 to 2
- post_scale: float32 [2688], replicated, may hold values from 0.5 to 2
- doc_starts: int32 [64], P('groups'), parts along dimension 0, may hold values from 0 to 4096, as said below
Outputs:
- hidden: bfloat16 [8192, 2688], P(('groups', 'seq')), parts along dimension 0
- pooled: float32 [64, 2688], P(('groups', 'seq')), parts along dimension 0
The draws below stay inside these ranges and needn't reach their ends.
There are 2 independent parts, one for each index of `groups`. The reference program is written for one: setup_inputs(seed, part) draws one part's arguments, and reference() takes and returns one part's arrays. A program takes and returns all parts, laid end to end along the dimension named above; an argument that names none is the same for every part. Nothing has to cross between parts.
Inputs may be any that keep to these rules, and one draw needn't show every extreme that they name: `doc_starts`: entries k * 2 to (k + 1) * 2 - 1 hold, rising, the positions in [k * 256, (k + 1) * 256) at which documents start, followed by (k + 1) * 256 in unused entries. Entry 0 is 0. Some device has 2 starts.
All inputs are finite; a program needn't handle non-finite values.
Results may differ from the reference program's by a relative error of at most 0.0051.
Values may be sent and summed in bfloat16 or wider, within the bound.
No kernel may reach another device: no remote copies, remote signals or barrier semaphores. Data moves between devices by JAX's collectives and lax.ppermute only.
A program may use at most 64 MiB of HBM per device.

```python
import math
import jax
import jax.numpy as jnp
from jax import lax

D = 2688
QUERY_HEADS = 16
KEY_VALUE_HEADS = 8
HEAD_FEATURES = 128
WINDOW_SPAN = 1024
SLOTS = 2
TOK_DEV = 256
PACKED_TOKENS = 4096
N_SEQ = 16


def truncated_gaussian(key, shape):
    return jnp.clip(jax.random.normal(key, shape, jnp.float32), -6.0, 6.0)


def key_visibility(key):
    return truncated_gaussian(jax.random.fold_in(key, 11), (PACKED_TOKENS, KEY_VALUE_HEADS * HEAD_FEATURES))


def draw_keys(key, part):
    visibility_grid = key_visibility(key)
    return visibility_grid.astype(jnp.bfloat16)


def draw_queries(key, part):
    base = truncated_gaussian(jax.random.fold_in(key, 14), (PACKED_TOKENS, QUERY_HEADS * HEAD_FEATURES))
    return base.astype(jnp.bfloat16)


def draw_out_weight(key, part):
    random_jitter = truncated_gaussian(jax.random.fold_in(key, 21), (QUERY_HEADS * HEAD_FEATURES, D))
    column_log = jax.random.uniform(jax.random.fold_in(key, 22), (1, D), jnp.float32, -1.2, 1.1)
    scaled = random_jitter * jnp.exp(column_log) * (QUERY_HEADS * HEAD_FEATURES) ** (-0.5)
    return scaled.astype(jnp.bfloat16)


def draw_doc_starts(key, part):
    device_ids = jnp.arange(N_SEQ, dtype=jnp.int32)
    pick = jax.random.randint(jax.random.fold_in(key, 31), (N_SEQ,), 0, 10)
    counts = jnp.where(pick < 4, 0, jnp.where(pick < 7, 1, 2))
    forced = jax.random.randint(jax.random.fold_in(key, 32), (), 0, N_SEQ)
    counts = jnp.where(device_ids == forced, 2, counts)
    counts = jnp.where(device_ids == 0, jnp.maximum(counts, 1), counts)
    half_rows = TOK_DEV // 2
    first_half = jax.random.randint(jax.random.fold_in(key, 33), (N_SEQ,), 0, half_rows)
    second_half = jax.random.randint(jax.random.fold_in(key, 34), (N_SEQ,), half_rows, TOK_DEV)
    single = jax.random.randint(jax.random.fold_in(key, 35), (N_SEQ,), 0, TOK_DEV)
    first_half = jnp.where(device_ids == 0, 0, first_half)
    single = jnp.where(device_ids == 0, 0, single)
    slot_first = jnp.where(counts == 2, first_half, jnp.where(counts == 1, single, TOK_DEV))
    slot_second = jnp.where(counts == 2, second_half, TOK_DEV)
    local_rows = jnp.stack([slot_first, slot_second], axis=1)
    return (device_ids[:, None] * TOK_DEV + local_rows).reshape(N_SEQ * SLOTS).astype(jnp.int32)


def block_scale(rng, extent, shards, smallest, largest):
    factor_of = 1.0
    for axis_at, parts in shards:
        draws = jax.random.uniform(jax.random.fold_in(jax.random.fold_in(rng, 6), axis_at), (parts,), jnp.float32, smallest / len(shards), largest / len(shards))
        factor_of = factor_of * jnp.repeat(jnp.exp(draws), extent[axis_at] // parts).reshape((-1,) + (1,) * (len(extent) - 1 - axis_at))
    return factor_of


def noise(stream_key, extent, width, most, split=(), kind=jnp.bfloat16):
    values = jax.random.normal(stream_key, extent, jnp.float32) * width
    if len(split) > 0:
        values = block_scale(stream_key, extent, split, -0.22, 0.18) * values
    return jnp.clip(values, min=-most, max=most).astype(kind)


def setup_inputs(seed: int = 0, part: int = 0) -> dict:
    splits = jax.random.split(jax.random.key(seed), 8)
    part_keys = jax.random.split(jax.random.fold_in(splits[7], part), 8)
    queries = draw_queries(jax.random.fold_in(jax.random.fold_in(splits[7], part), 71), part)
    keys = draw_keys(jax.random.fold_in(jax.random.fold_in(splits[7], part), 71), part)
    values = noise(part_keys[2], (PACKED_TOKENS, KEY_VALUE_HEADS * HEAD_FEATURES), 1.0, 6.0, ((0, 16),))
    residual = noise(part_keys[3], (PACKED_TOKENS, D), 1.0, 6.0, ((0, 16),))
    out_weight = draw_out_weight(jax.random.fold_in(splits[7], 71), part)
    post_scale = jnp.clip(jnp.exp(jax.random.uniform(splits[5], (D,), jnp.float32, math.log(0.5), math.log(2.0))), 0.5, 2.0)
    doc_starts = draw_doc_starts(jax.random.fold_in(jax.random.fold_in(splits[7], part), 71), part)
    return dict(queries=queries, keys=keys, values=values, residual=residual, out_weight=out_weight, post_scale=post_scale, doc_starts=doc_starts)


query_scale = 168.0 ** (-0.5)
norm_eps = 1e-06

def reference(queries, keys, values, residual, out_weight, post_scale, doc_starts):
    queries_each_group = QUERY_HEADS // KEY_VALUE_HEADS
    slot_count = N_SEQ * SLOTS
    slot_ids = jnp.arange(slot_count, dtype=jnp.int32)
    live_slot = doc_starts < (slot_ids // SLOTS + 1) * TOK_DEV
    block_row_slab = math.gcd(PACKED_TOKENS, 512)
    key_total = WINDOW_SPAN + block_row_slab
    key_with_margin = jnp.concatenate([jnp.zeros((WINDOW_SPAN, KEY_VALUE_HEADS * HEAD_FEATURES), keys.dtype), keys], axis=0)
    value_with_margin = jnp.concatenate([jnp.zeros((WINDOW_SPAN, KEY_VALUE_HEADS * HEAD_FEATURES), values.dtype), values], axis=0)

    def one_block(slot_sums, first_row):
        query_pos = first_row + jnp.arange(block_row_slab, dtype=jnp.int32)
        earlier_starts = live_slot[None, :] & (doc_starts[None, :] <= query_pos[:, None])
        last_start = lax.optimization_barrier(jnp.max(jnp.where(earlier_starts, doc_starts[None, :], 0), axis=1))
        slot_owner = lax.optimization_barrier(jnp.max(jnp.where(earlier_starts, slot_ids[None, :], -1), axis=1))
        lowest_key = jnp.maximum(last_start, query_pos - WINDOW_SPAN + 1)
        key_pos = first_row - WINDOW_SPAN + jnp.arange(key_total, dtype=jnp.int32)
        query_matrix = lax.dynamic_slice_in_dim(queries, first_row, block_row_slab, 0).astype(jnp.float32)
        query_matrix = query_matrix.reshape(block_row_slab, KEY_VALUE_HEADS, queries_each_group, HEAD_FEATURES)
        key_matrix = lax.dynamic_slice_in_dim(key_with_margin, first_row, key_total, 0).astype(jnp.float32)
        key_matrix = key_matrix.reshape(key_total, KEY_VALUE_HEADS, HEAD_FEATURES)
        value_matrix = lax.dynamic_slice_in_dim(value_with_margin, first_row, key_total, 0).astype(jnp.float32)
        value_matrix = value_matrix.reshape(key_total, KEY_VALUE_HEADS, HEAD_FEATURES)
        scores = jnp.einsum('qgrd,kgd->qgrk', query_matrix, key_matrix) * query_scale
        visible = (key_pos[None, :] >= lowest_key[:, None]) & (key_pos[None, :] <= query_pos[:, None])
        scores = jnp.where(visible[:, None, None, :], scores, -jnp.inf)
        row_peak = lax.optimization_barrier(jnp.max(scores, axis=3, keepdims=True))
        raised = jnp.exp(scores - row_peak)
        totals = lax.optimization_barrier(jnp.sum(raised, axis=3, keepdims=True))
        weights = lax.optimization_barrier(raised.astype(jnp.bfloat16)).astype(jnp.float32)
        weighted = jnp.einsum('qgrk,kgd->qgrd', weights, value_matrix)
        attended = (weighted / totals).astype(jnp.bfloat16).reshape(block_row_slab, QUERY_HEADS * HEAD_FEATURES)
        projected = jnp.dot(attended, out_weight, preferred_element_type=jnp.float32)
        mean_square = lax.optimization_barrier(jnp.mean(projected * projected, axis=1, keepdims=True))
        resid_rows = lax.dynamic_slice_in_dim(residual, first_row, block_row_slab, 0).astype(jnp.float32)
        updated = resid_rows + projected * lax.rsqrt(mean_square + norm_eps) * post_scale[None, :]
        member = (slot_owner[:, None] == slot_ids[None, :]).astype(jnp.float32)
        slot_sums = slot_sums + jnp.dot(member.T, updated, precision=lax.Precision.HIGHEST)
        return (slot_sums, updated.astype(jnp.bfloat16))
    firsts = jnp.arange(0, PACKED_TOKENS, block_row_slab, dtype=jnp.int32)
    slot_sums, hidden_blocks = lax.scan(one_block, jnp.zeros((slot_count, D), jnp.float32), firsts)
    hidden = hidden_blocks.reshape(PACKED_TOKENS, D)
    later_starts = live_slot[None, :] & (doc_starts[None, :] > doc_starts[:, None])
    following = lax.optimization_barrier(jnp.min(jnp.where(later_starts, doc_starts[None, :], PACKED_TOKENS), axis=1))
    doc_length = jnp.maximum(following - doc_starts, 1).astype(jnp.float32)
    pooled = jnp.where(live_slot[:, None], slot_sums / doc_length[:, None], 0.0)
    return (hidden, pooled)
```

```python
import math

import jax
import jax.numpy as jnp
from jax import lax
from jax.experimental import pallas as pl
from jax.experimental.pallas import tpu as pltpu
from jax.sharding import PartitionSpec as P

HEAD_FEATURES = 128
WINDOW_SPAN = 1024
SLOTS = 2
LANES = 128
UNUSED = 2**30

query_scale = 168.0 ** (-0.5)
norm_eps = 1e-06


def chip_grid(mesh):
    devices = mesh.devices.reshape(mesh.shape["groups"], mesh.shape["seq"])
    where = [(*d.coords, d.core_on_chip) for d in devices[0]]
    xs = len({w[0] for w in where})
    zs = len({w[2] for w in where})
    if xs * zs * 2 != len(where):
        return None
    return zs, xs


def passed_along(block, axis, distance):
    devices = range(lax.axis_size(axis))
    route = [(i - distance, i) for i in devices if i - distance in devices]
    return lax.ppermute(block, axis, route)


def moved(block, grid, step):
    zs, xs = grid
    route = []
    for z in range(zs):
        for x in range(xs):
            for c in range(2):
                to = step(z, x, c)
                if to is not None:
                    route.append(((z * xs + x) * 2 + c, (to[0] * xs + to[1]) * 2 + to[2]))
    return lax.ppermute(block, "seq", route)


def last_start_at(pos, prev, s0, s1):
    last = jnp.maximum(prev, jnp.where(s0 <= pos, s0, 0))
    return jnp.maximum(last, jnp.where(s1 <= pos, s1, 0))


def attend(meta, queries, key_blocks, value_blocks, block_at):
    rows, width = queries.shape
    kv_width = key_blocks[0].shape[1]
    heads = kv_width // HEAD_FEATURES
    each = width // kv_width
    count = len(key_blocks)
    to_exp2 = query_scale * math.log2(math.e)

    def kernel(meta, q_ref, *refs):
        k_refs, v_refs = refs[:count], refs[count : 2 * count]
        out_ref, bias, s_ref, m_ref, l_ref, acc = refs[2 * count :]
        first = meta[0] * rows
        prev, s0, s1 = meta[1], meta[2], meta[3]
        lowest = jnp.maximum(last_start_at(first, prev, s0, s1), first - WINDOW_SPAN + 1)
        places = []
        for b in range(count):
            index, valid = block_at(b, meta[0])
            start = index * rows
            places.append((start, valid & (index >= 0) & (start + rows > lowest)))

        @pl.when(pl.program_id(0) == 0)
        def _():
            for b, (start, need) in enumerate(places):

                @pl.when(need)
                def _():
                    q_pos = first + lax.broadcasted_iota(jnp.int32, (rows, rows), 0)
                    k_pos = start + lax.broadcasted_iota(jnp.int32, (rows, rows), 1)
                    low = last_start_at(q_pos, prev, s0, s1)
                    low = jnp.maximum(low, q_pos - WINDOW_SPAN + 1)
                    visible = (k_pos >= low) & (k_pos <= q_pos)
                    bias[b] = jnp.where(visible, 0.0, -jnp.inf)

        q = jnp.concatenate(
            [q_ref[:, r * HEAD_FEATURES : (r + 1) * HEAD_FEATURES] for r in range(each)], axis=0
        )
        m_ref[...] = jnp.full(m_ref.shape, -jnp.inf, jnp.float32)
        l_ref[...] = jnp.zeros(l_ref.shape, jnp.float32)
        acc[...] = jnp.zeros(acc.shape, jnp.float32)
        for b, (start, need) in enumerate(places):

            @pl.when(need)
            def _():
                s = lax.dot_general(
                    q, k_refs[b][...], (((1,), (1,)), ((), ())), preferred_element_type=jnp.float32
                )
                s = s + jnp.concatenate([bias[b]] * each, axis=0)
                s_ref[b] = s
                m_ref[...] = jnp.maximum(m_ref[...], jnp.max(s, axis=1, keepdims=True))

        for b, (start, need) in enumerate(places):

            @pl.when(need)
            def _():
                p = jnp.exp2((s_ref[b] - m_ref[...]) * to_exp2)
                l_ref[...] += jnp.sum(p, axis=1, keepdims=True)
                acc[...] += jnp.dot(
                    p.astype(jnp.bfloat16), v_refs[b][...], preferred_element_type=jnp.float32
                )

        result = (acc[...] / l_ref[...]).astype(jnp.bfloat16)
        for r in range(each):
            out_ref[:, r * HEAD_FEATURES : (r + 1) * HEAD_FEATURES] = result[
                r * rows : (r + 1) * rows
            ]

    q_spec = pl.BlockSpec((rows, each * HEAD_FEATURES), lambda g, meta: (0, g))
    kv_spec = pl.BlockSpec((rows, HEAD_FEATURES), lambda g, meta: (0, g))
    return pl.pallas_call(
        kernel,
        grid_spec=pltpu.PrefetchScalarGridSpec(
            num_scalar_prefetch=1,
            grid=(heads,),
            in_specs=[q_spec] + [kv_spec] * (2 * count),
            out_specs=q_spec,
            scratch_shapes=[
                pltpu.VMEM((count, rows, rows), jnp.float32),
                pltpu.VMEM((count, each * rows, rows), jnp.float32),
                pltpu.VMEM((each * rows, 1), jnp.float32),
                pltpu.VMEM((each * rows, 1), jnp.float32),
                pltpu.VMEM((each * rows, HEAD_FEATURES), jnp.float32),
            ],
        ),
        out_shape=jax.ShapeDtypeStruct(queries.shape, jnp.bfloat16),
        name="attend",
    )(meta, queries, *key_blocks, *value_blocks)


def project(meta, attended, residual, post_scale, pieces, offsets, seq_size):
    rows, width = attended.shape
    columns = residual.shape[1]
    count = len(pieces)
    tiles = columns // LANES
    padded = -(-tiles // 8) * 8
    split = next(n for n in (3, 2, 1) if tiles % n == 0) * LANES
    starts = range(0, columns, split)

    def kernel(meta, offs, att_ref, res_ref, post_ref, *refs):
        piece_refs = refs[:count]
        hidden_ref, sums_ref, send_ref, w_ref, proj, sems = refs[count:]
        copies = []
        for i, ref in enumerate(piece_refs):
            tall = ref.shape[0]
            at = pl.multiple_of(offs[i], math.gcd(tall, 16))
            copies.append(
                pltpu.make_async_copy(ref, w_ref.at[pl.ds(at, tall)], sems.at[i])
            )
        for copy in copies:
            copy.start()
        first = meta[0] * rows
        prev, s0, s1 = meta[1], meta[2], meta[3]
        send_ref[...] = jnp.zeros(send_ref.shape, jnp.float32)
        pos = first + lax.broadcasted_iota(jnp.int32, (8, rows), 1)
        line = lax.broadcasted_iota(jnp.int32, (8, rows), 0)
        last = last_start_at(pos, prev, s0, s1)
        masks = (
            ((line == 0) & (last == s0)) | ((line == 1) & (last == s1)) | ((line == 2) & (last < first))
        ).astype(jnp.float32)
        for copy in copies:
            copy.wait()
        square = jnp.zeros((rows, 1), jnp.float32)
        for at in starts:
            part = jnp.dot(
                att_ref[...], w_ref[:, at : at + split], preferred_element_type=jnp.float32
            )
            proj[:, at : at + split] = part
            square = square + jnp.sum(part * part, axis=1, keepdims=True)
        norm = lax.rsqrt(square * (1.0 / columns) + norm_eps)
        owner = prev // rows
        for at in starts:
            updated = res_ref[:, at : at + split].astype(jnp.float32) + (
                proj[:, at : at + split] * norm * post_ref[:, at : at + split]
            )
            hidden_ref[:, at : at + split] = updated.astype(jnp.bfloat16)
            sums = jnp.dot(
                masks, updated, precision=lax.Precision.HIGHEST, preferred_element_type=jnp.float32
            )
            sums_ref[:, at : at + split] = sums
            for t in range(split // LANES):
                send_ref[pl.ds(owner, 1), at // LANES + t, :] = sums[
                    2:3, t * LANES : (t + 1) * LANES
                ]

    whole = pl.BlockSpec(memory_space=pltpu.MemorySpace.VMEM)
    smem = pl.BlockSpec(memory_space=pltpu.MemorySpace.SMEM)
    return pl.pallas_call(
        kernel,
        in_specs=[smem, smem, whole, whole, whole] + [pl.BlockSpec(memory_space=pl.ANY)] * count,
        out_specs=(whole, whole, whole),
        out_shape=(
            jax.ShapeDtypeStruct((rows, columns), jnp.bfloat16),
            jax.ShapeDtypeStruct((8, columns), jnp.float32),
            jax.ShapeDtypeStruct((seq_size, padded, LANES), jnp.float32),
        ),
        scratch_shapes=[
            pltpu.VMEM((width, columns), jnp.bfloat16),
            pltpu.VMEM((rows, columns), jnp.float32),
            pltpu.SemaphoreType.DMA((count,)),
        ],
        name="project",
    )(meta, offsets, attended, residual, post_scale[None, :], *pieces)


def body(grid, queries, keys, values, residual, out_weight, post_scale, doc_starts):
    seq_size = lax.axis_size("seq")
    my_index = lax.axis_index("seq")
    tok_rows = queries.shape[0]
    halo_blocks = WINDOW_SPAN // tok_rows
    part_rows = out_weight.shape[0]
    by_links = (
        grid is not None
        and grid[1] == 2
        and halo_blocks == 4
        and lax.axis_size("groups") == 2
        and grid[0] == 4
        and part_rows % 32 == 0
    )

    slot_count = doc_starts.shape[0]
    slot_ids = jnp.arange(slot_count, dtype=jnp.int32)
    live_slot = doc_starts < (slot_ids // SLOTS + 1) * tok_rows
    first = my_index * tok_rows
    my_starts = lax.dynamic_slice_in_dim(doc_starts, my_index * SLOTS, SLOTS)
    my_live = my_starts < first + tok_rows
    prev = jnp.max(jnp.where(live_slot & (doc_starts < first), doc_starts, 0))
    shown = jnp.where(my_live, my_starts, UNUSED)
    meta = jnp.concatenate([my_index[None], prev[None], shown]).astype(jnp.int32)

    if by_links:
        zs, xs = grid
        half_rows = part_rows // 2
        z, x, c = my_index // 4, my_index // 2 % 2, my_index % 2
        y = lax.axis_index("groups")

        def turned(block, k):
            return moved(block, grid, lambda z, x, c: ((z + k) % zs, x, c))

        def over_x(block):
            return moved(block, grid, lambda z, x, c: (z, 1 - x, c))

        def over_c(block):
            return moved(block, grid, lambda z, x, c: (z, x, 1 - c))

        def over_y(block):
            return lax.ppermute(block, "groups", [(0, 1), (1, 0)])

        def up(block):
            return moved(block, grid, lambda z, x, c: (z + 1, x, c) if z + 1 < zs else None)

        own = lax.dynamic_slice_in_dim(out_weight, y * half_rows, half_rows)
        direct = [(over_x(own), z, 1 - x)]
        for k in (1, 3, 2):
            ring = turned(own, k)
            direct.append((ring, (z - k) % zs, x))
            direct.append((over_x(ring), (z - k) % zs, 1 - x))
        pieces, offsets = [], []

        def place(piece, z, x, c, half):
            pieces.append(piece)
            offsets.append(((z * xs + x) * 2 + c) * part_rows + half * half_rows)

        place(out_weight, z, x, c, 0)
        place(over_c(out_weight), z, x, 1 - c, 0)
        for piece, pz, px in direct:
            other = over_y(piece)
            place(piece, pz, px, c, y)
            place(other, pz, px, c, 1 - y)
            place(over_c(piece), pz, px, 1 - c, y)
            place(over_c(other), pz, px, 1 - c, 1 - y)
        offsets = jnp.stack(offsets).astype(jnp.int32)

        groups = []
        for mine in (keys, values):
            below = up(mine)
            aside = over_x(jnp.where(x == 0, mine, below))
            groups.append(
                [
                    mine,
                    moved(mine, grid, lambda z, x, c: (z, x, 1) if c == 0 else None),
                    below,
                    moved(below, grid, lambda z, x, c: (z, x, 0) if c == 1 else None),
                    aside,
                    over_c(aside),
                ]
            )
        key_blocks, value_blocks = groups

        def block_at(b, index):
            chip, core = index // 2, index % 2
            back = (0, 0, 2, 2, 1, 1)[b]
            place = (chip - back) * 2 + (core if b % 2 == 0 else 1 - core)
            valid = True
            if b == 1:
                valid = core == 1
            if b == 3:
                valid = core == 0
            return place, (place <= index) & valid
    else:
        pieces = [lax.all_gather(out_weight, "seq", axis=0, tiled=True)]
        offsets = jnp.zeros((1,), jnp.int32)
        key_blocks, value_blocks = [keys], [values]
        for distance in range(1, halo_blocks + 1):
            key_blocks.append(passed_along(keys, "seq", distance))
            value_blocks.append(passed_along(values, "seq", distance))

        def block_at(b, index):
            return index - b, index >= b

    attended = attend(meta, queries, key_blocks, value_blocks, block_at)
    hidden, slot_sums, send = project(
        meta, attended, residual, post_scale, pieces, offsets, seq_size
    )
    arrived = lax.all_to_all(send, "seq", 0, 0, tiled=True)
    columns = residual.shape[1]
    carried_sum = jnp.sum(arrived, axis=0).reshape(-1)[:columns]
    last_live = jnp.sum(my_live.astype(jnp.int32)) - 1
    tail_pick = (jnp.arange(SLOTS, dtype=jnp.int32) == last_live).astype(jnp.float32)
    doc_sums = slot_sums[:SLOTS] + tail_pick[:, None] * carried_sum[None, :]
    total_tokens = tok_rows * seq_size
    later_starts = live_slot[None, :] & (doc_starts[None, :] > my_starts[:, None])
    following = jnp.min(jnp.where(later_starts, doc_starts[None, :], total_tokens), axis=1)
    doc_length = jnp.maximum(following - my_starts, 1).astype(jnp.float32)
    pooled = jnp.where(my_live[:, None], doc_sums / doc_length[:, None], 0.0)
    return (hidden, pooled)


def solution(mesh):
    grid = chip_grid(mesh)
    placed = (
        P(("groups", "seq"), None),
        P(("groups", "seq"), None),
        P(("groups", "seq"), None),
        P(("groups", "seq"), None),
        P("seq", None),
        P(),
        P("groups"),
    )

    def whole(*args):
        return body(grid, *args)

    return jax.shard_map(
        whole,
        mesh=mesh,
        in_specs=placed,
        out_specs=(P(("groups", "seq"), None), P(("groups", "seq"), None)),
        check_vma=False,
    )
```

```python
import math

import jax
import jax.numpy as jnp
from jax import lax
from jax.experimental import pallas as pl
from jax.experimental.pallas import tpu as pltpu
from jax.sharding import PartitionSpec as P


HEAD_FEATURES = 128
WINDOW_SPAN = 1024
SLOTS = 2
LANES = 128
UNUSED = 2**30

query_scale = 168.0 ** (-0.5)
norm_eps = 1e-06


def chip_grid(mesh):
    devices = mesh.devices.reshape(mesh.shape["groups"], mesh.shape["seq"])
    where = [(*d.coords, d.core_on_chip) for d in devices[0]]
    xs = len({w[0] for w in where})
    zs = len({w[2] for w in where})
    if xs * zs * 2 != len(where):
        return None
    return zs, xs


def passed_along(block, axis, distance):
    devices = range(lax.axis_size(axis))
    route = [(i - distance, i) for i in devices if i - distance in devices]
    return lax.ppermute(block, axis, route)


def moved(block, grid, step):
    zs, xs = grid
    route = []
    for z in range(zs):
        for x in range(xs):
            for c in range(2):
                to = step(z, x, c)
                if to is not None:
                    route.append(((z * xs + x) * 2 + c, (to[0] * xs + to[1]) * 2 + to[2]))
    return lax.ppermute(block, "seq", route)


def last_start_at(pos, prev, s0, s1):
    last = jnp.maximum(prev, jnp.where(s0 <= pos, s0, 0))
    return jnp.maximum(last, jnp.where(s1 <= pos, s1, 0))


def attend(meta, queries, key_blocks, value_blocks, block_at, heads_from, heads_to, per_step):
    rows, width = queries.shape
    kv_width = key_blocks[0].shape[1]
    each = width // kv_width
    count = len(key_blocks)
    tall = each * rows
    to_exp2 = query_scale * math.log2(math.e)
    steps = (heads_to - heads_from) // per_step
    skip = heads_from // per_step

    def kernel(meta, q_ref, *refs):
        k_refs, v_refs = refs[:count], refs[count : 2 * count]
        out_ref, bias, s_ref, m_ref, l_ref, acc = refs[2 * count :]
        first = meta[0] * rows
        prev, s0, s1 = meta[1], meta[2], meta[3]
        lowest = jnp.maximum(last_start_at(first, prev, s0, s1), first - WINDOW_SPAN + 1)
        places = []
        for b in range(count):
            index, valid = block_at(b, meta[0])
            start = index * rows
            places.append((start, valid & (index >= 0) & (start + rows > lowest)))

        @pl.when(pl.program_id(0) == 0)
        def _():
            for b, (start, need) in enumerate(places):

                @pl.when(need)
                def _():
                    q_pos = first + lax.broadcasted_iota(jnp.int32, (rows, rows), 0)
                    k_pos = start + lax.broadcasted_iota(jnp.int32, (rows, rows), 1)
                    low = last_start_at(q_pos, prev, s0, s1)
                    low = jnp.maximum(low, q_pos - WINDOW_SPAN + 1)
                    visible = (k_pos >= low) & (k_pos <= q_pos)
                    bias[b] = jnp.where(visible, 0.0, -jnp.inf)

        m_ref[...] = jnp.full(m_ref.shape, -jnp.inf, jnp.float32)
        l_ref[...] = jnp.zeros(l_ref.shape, jnp.float32)
        acc[...] = jnp.zeros(acc.shape, jnp.float32)

        def lanes(block):
            return [block[:, t : t + LANES] for t in range(0, rows, LANES)]

        for b, (start, need) in enumerate(places):

            @pl.when(need)
            def _():
                for g in range(per_step):
                    k = k_refs[b][:, g * HEAD_FEATURES : (g + 1) * HEAD_FEATURES]
                    for r in range(each):
                        at = (g * each + r) * HEAD_FEATURES
                        s = lax.dot_general(
                            q_ref[:, at : at + HEAD_FEATURES], k,
                            (((1,), (1,)), ((), ())), preferred_element_type=jnp.float32,
                        )
                        s = s + bias[b]
                        s_ref[b, g, r * rows : (r + 1) * rows] = s
                        top = m_ref[g, r * rows : (r + 1) * rows]
                        for part in lanes(s):
                            top = jnp.maximum(top, part)
                        m_ref[g, r * rows : (r + 1) * rows] = top

        for g in range(per_step):
            peak = jnp.max(m_ref[g], axis=1, keepdims=True)
            m_ref[g] = jnp.broadcast_to(peak, (tall, LANES))

        for b, (start, need) in enumerate(places):

            @pl.when(need)
            def _():
                for g in range(per_step):
                    peak = m_ref[g]
                    parts = [jnp.exp2((part - peak) * to_exp2) for part in lanes(s_ref[b, g])]
                    l_ref[g] += sum(parts[1:], parts[0])
                    p = jnp.concatenate([part.astype(jnp.bfloat16) for part in parts], axis=1)
                    acc[g] += jnp.dot(
                        p,
                        v_refs[b][:, g * HEAD_FEATURES : (g + 1) * HEAD_FEATURES],
                        preferred_element_type=jnp.float32,
                    )

        for g in range(per_step):
            totals = jnp.sum(l_ref[g], axis=1, keepdims=True)
            result = (acc[g] / totals).astype(jnp.bfloat16)
            for r in range(each):
                at = (g * each + r) * HEAD_FEATURES
                out_ref[:, at : at + HEAD_FEATURES] = result[r * rows : (r + 1) * rows]

    q_spec = pl.BlockSpec((rows, per_step * each * HEAD_FEATURES), lambda g, meta: (0, g + skip))
    kv_spec = pl.BlockSpec((rows, per_step * HEAD_FEATURES), lambda g, meta: (0, g + skip))
    out_spec = pl.BlockSpec((rows, per_step * each * HEAD_FEATURES), lambda g, meta: (0, g))
    return pl.pallas_call(
        kernel,
        grid_spec=pltpu.PrefetchScalarGridSpec(
            num_scalar_prefetch=1,
            grid=(steps,),
            in_specs=[q_spec] + [kv_spec] * (2 * count),
            out_specs=out_spec,
            scratch_shapes=[
                pltpu.VMEM((count, rows, rows), jnp.float32),
                pltpu.VMEM((count, per_step, tall, rows), jnp.float32),
                pltpu.VMEM((per_step, tall, LANES), jnp.float32),
                pltpu.VMEM((per_step, tall, LANES), jnp.float32),
                pltpu.VMEM((per_step, tall, HEAD_FEATURES), jnp.float32),
            ],
        ),
        out_shape=jax.ShapeDtypeStruct((rows, steps * per_step * each * HEAD_FEATURES), jnp.bfloat16),
        name="attend",
    )(meta, queries, *key_blocks, *value_blocks)


def gathered(refs, w_ref, offs, sems):
    copies = []
    for i, ref in enumerate(refs):
        tall = ref.shape[0]
        at = pl.multiple_of(offs[i], math.gcd(tall, 16))
        copies.append(pltpu.make_async_copy(ref, w_ref.at[pl.ds(at, tall)], sems.at[i]))
    return copies


def column_split(columns):
    tiles = columns // LANES
    return next(n for n in (3, 2, 1) if tiles % n == 0) * LANES


def project_early(chunk_at, attended, pieces, offsets, chunk):
    rows = attended.shape[0]
    columns = pieces[0].shape[1]
    count = len(pieces)
    chunks = chunk_at.shape[0]
    split = column_split(columns)

    def kernel(chunk_at, offs, att_ref, *refs):
        piece_refs = refs[:count]
        out_ref, w_ref, att, sems = refs[count:]
        copies = gathered(piece_refs, w_ref, offs, sems)
        for copy in copies:
            copy.start()
        for i in range(chunks):
            at = pl.multiple_of(chunk_at[i] * chunk, LANES)
            att[:, i * chunk : (i + 1) * chunk] = att_ref[:, pl.ds(at, chunk)]
        for copy in copies:
            copy.wait()
        for at in range(0, columns, split):
            out_ref[:, at : at + split] = jnp.dot(
                att[...], w_ref[:, at : at + split], preferred_element_type=jnp.float32
            )

    whole = pl.BlockSpec(memory_space=pltpu.MemorySpace.VMEM)
    smem = pl.BlockSpec(memory_space=pltpu.MemorySpace.SMEM)
    return pl.pallas_call(
        kernel,
        in_specs=[smem, smem, whole] + [pl.BlockSpec(memory_space=pl.ANY)] * count,
        out_specs=whole,
        out_shape=jax.ShapeDtypeStruct((rows, columns), jnp.float32),
        scratch_shapes=[
            pltpu.VMEM((chunks * chunk, columns), jnp.bfloat16),
            pltpu.VMEM((rows, chunks * chunk), jnp.bfloat16),
            pltpu.SemaphoreType.DMA((count,)),
        ],
        name="project_early",
    )(chunk_at, offsets, attended, *pieces)


def project(meta, chunk_at, chunk, attended, partial, residual, post_scale, pieces, offsets, seq_size):
    rows = attended.shape[0]
    columns = residual.shape[1]
    count = len(pieces)
    tiles = columns // LANES
    padded = -(-tiles // 8) * 8
    split = column_split(columns)
    starts = range(0, columns, split)
    partials = [] if partial is None else [partial]

    def kernel(meta, chunk_at, offs, att_ref, res_ref, post_ref, *refs):
        part_refs, refs = refs[: len(partials)], refs[len(partials) :]
        piece_refs = refs[:count]
        hidden_ref, sums_ref, send_ref, w_ref, proj, sems = refs[count:]
        copies = gathered(piece_refs, w_ref, offs, sems)
        for copy in copies:
            copy.start()
        first = meta[0] * rows
        prev, s0, s1 = meta[1], meta[2], meta[3]
        send_ref[...] = jnp.zeros(send_ref.shape, jnp.float32)
        pos = first + lax.broadcasted_iota(jnp.int32, (8, rows), 1)
        line = lax.broadcasted_iota(jnp.int32, (8, rows), 0)
        last = last_start_at(pos, prev, s0, s1)
        masks = (
            ((line == 0) & (last == s0)) | ((line == 1) & (last == s1)) | ((line == 2) & (last < first))
        ).astype(jnp.float32)
        att = att_ref[:, pl.ds(pl.multiple_of(chunk_at[0] * chunk, LANES), chunk)]
        for copy in copies:
            copy.wait()
        square = jnp.zeros((rows, LANES), jnp.float32)
        for at in starts:
            part = jnp.dot(att, w_ref[:, at : at + split], preferred_element_type=jnp.float32)
            for ref in part_refs:
                part = part + ref[:, at : at + split]
            proj[:, at : at + split] = part
            for t in range(0, split, LANES):
                square = square + part[:, t : t + LANES] * part[:, t : t + LANES]
        total = jnp.sum(square, axis=1, keepdims=True)
        norm = jnp.broadcast_to(lax.rsqrt(total * (1.0 / columns) + norm_eps), (rows, LANES))
        norm = jnp.concatenate([norm] * (split // LANES), axis=1)
        owner = prev // rows
        for at in starts:
            updated = res_ref[:, at : at + split].astype(jnp.float32) + (
                proj[:, at : at + split] * norm * post_ref[:, at : at + split]
            )
            hidden_ref[:, at : at + split] = updated.astype(jnp.bfloat16)
            sums = jnp.dot(
                masks, updated, precision=lax.Precision.HIGHEST, preferred_element_type=jnp.float32
            )
            sums_ref[:, at : at + split] = sums
            for t in range(split // LANES):
                send_ref[pl.ds(owner, 1), at // LANES + t, :] = sums[
                    2:3, t * LANES : (t + 1) * LANES
                ]

    whole = pl.BlockSpec(memory_space=pltpu.MemorySpace.VMEM)
    smem = pl.BlockSpec(memory_space=pltpu.MemorySpace.SMEM)
    return pl.pallas_call(
        kernel,
        in_specs=[smem, smem, smem, whole, whole, whole]
        + [whole] * len(partials)
        + [pl.BlockSpec(memory_space=pl.ANY)] * count,
        out_specs=(whole, whole, whole),
        out_shape=(
            jax.ShapeDtypeStruct((rows, columns), jnp.bfloat16),
            jax.ShapeDtypeStruct((8, columns), jnp.float32),
            jax.ShapeDtypeStruct((seq_size, padded, LANES), jnp.float32),
        ),
        scratch_shapes=[
            pltpu.VMEM((chunk, columns), jnp.bfloat16),
            pltpu.VMEM((rows, columns), jnp.float32),
            pltpu.SemaphoreType.DMA((count,)),
        ],
        name="project",
    )(meta, chunk_at, offsets, attended, residual, post_scale[None, :], *partials, *pieces)


def by_links(grid, groups, tok_rows, part_rows):
    return grid == (4, 2) and groups == 2 and WINDOW_SPAN == 4 * tok_rows and part_rows % 32 == 0


def body(grid, queries, keys, values, residual, out_weight, post_scale, doc_starts):
    seq_size = lax.axis_size("seq")
    my_index = lax.axis_index("seq")
    tok_rows = queries.shape[0]
    halo_blocks = WINDOW_SPAN // tok_rows
    part_rows = out_weight.shape[0]
    kv_heads = keys.shape[1] // HEAD_FEATURES

    slot_count = doc_starts.shape[0]
    slot_ids = jnp.arange(slot_count, dtype=jnp.int32)
    live_slot = doc_starts < (slot_ids // SLOTS + 1) * tok_rows
    first = my_index * tok_rows
    my_starts = lax.dynamic_slice_in_dim(doc_starts, my_index * SLOTS, SLOTS)
    my_live = my_starts < first + tok_rows
    prev = jnp.max(jnp.where(live_slot & (doc_starts < first), doc_starts, 0))
    shown = jnp.where(my_live, my_starts, UNUSED)
    meta = jnp.concatenate([my_index[None], prev[None], shown]).astype(jnp.int32)

    if by_links(grid, lax.axis_size("groups"), tok_rows, part_rows):
        zs, xs = grid
        half_rows = part_rows // 2
        chunk = xs * 2 * part_rows
        z, x, c = my_index // 4, my_index // 2 % 2, my_index % 2
        y = lax.axis_index("groups")

        def turned(k):
            return lambda block: moved(block, grid, lambda z, x, c: ((z + k) % zs, x, c))

        def over_x(block):
            return moved(block, grid, lambda z, x, c: (z, 1 - x, c))

        def over_c(block):
            return moved(block, grid, lambda z, x, c: (z, x, 1 - c))

        def over_y(block):
            return lax.ppermute(block, "groups", [(0, 1), (1, 0)])

        def up(block):
            return moved(block, grid, lambda z, x, c: (z + 1, x, c) if z + 1 < zs else None)

        def right(block):
            return moved(block, grid, lambda z, x, c: (z, x, 1) if c == 0 else None)

        def left(block):
            return moved(block, grid, lambda z, x, c: (z, x, 0) if c == 1 else None)

        own = lax.dynamic_slice_in_dim(out_weight, y * half_rows, half_rows)
        early, late = ([], []), ([], [])

        def place(which, slot, piece, x, c, half):
            which[0].append(piece)
            which[1].append((slot * xs * 2 + x * 2 + c) * part_rows + half * half_rows)

        def place_all(which, slot, piece, x):
            other = over_y(piece)
            place(which, slot, piece, x, c, y)
            place(which, slot, other, x, c, 1 - y)
            place(which, slot, over_c(piece), x, 1 - c, y)
            place(which, slot, over_c(other), x, 1 - c, 1 - y)

        place(early, 0, out_weight, x, c, 0)
        place(early, 0, over_c(out_weight), x, 1 - c, 0)
        place_all(early, 0, over_x(own), 1 - x)
        for slot, k in ((1, 1), (2, 3), (0, 2)):
            which = late if k == 2 else early
            ring = turned(k)(own)
            place_all(which, slot, ring, x)
            place_all(which, slot, over_x(ring), 1 - x)
        early_at = jnp.stack([z, (z - 1) % zs, (z - 3) % zs]).astype(jnp.int32)
        late_at = ((z - 2) % zs)[None].astype(jnp.int32)
        early_offsets = jnp.stack([jnp.asarray(o, jnp.int32) for o in early[1]])
        late_offsets = jnp.stack([jnp.asarray(o, jnp.int32) for o in late[1]])

        groups = []
        for mine in (keys, values):
            below = up(mine)
            aside = over_x(jnp.where(x == 0, mine, below))
            groups.append([mine, right(mine), below, left(below), aside, over_c(aside)])
        key_blocks, value_blocks = groups

        def block_at(b, index):
            chip, core = index // 2, index % 2
            back = (0, 0, 2, 2, 1, 1)[b]
            place = (chip - back) * 2 + (core if b % 2 == 0 else 1 - core)
            valid = True
            if b == 1:
                valid = core == 1
            if b == 3:
                valid = core == 0
            return place, (place <= index) & valid

        attended = attend(
            meta, queries, key_blocks, value_blocks, block_at, 0, kv_heads, 4
        )
        partial = project_early(early_at, attended, early[0], early_offsets, chunk)
        pieces, offsets = late[0], late_offsets
    else:
        pieces = [lax.all_gather(out_weight, "seq", axis=0, tiled=True)]
        offsets = jnp.zeros((1,), jnp.int32)
        late_at, chunk, partial = offsets, out_weight.shape[0] * seq_size, None
        key_blocks, value_blocks = [keys], [values]
        for distance in range(1, halo_blocks + 1):
            key_blocks.append(passed_along(keys, "seq", distance))
            value_blocks.append(passed_along(values, "seq", distance))

        def block_at(b, index):
            return index - b, index >= b

        attended = attend(
            meta, queries, key_blocks, value_blocks, block_at, 0, kv_heads, math.gcd(kv_heads, 4)
        )

    hidden, slot_sums, send = project(
        meta, late_at, chunk, attended, partial, residual, post_scale, pieces, offsets, seq_size
    )
    arrived = lax.all_to_all(send, "seq", 0, 0, tiled=True)
    columns = residual.shape[1]
    carried_sum = jnp.sum(arrived, axis=0).reshape(-1)[:columns]
    last_live = jnp.sum(my_live.astype(jnp.int32)) - 1
    tail_pick = (jnp.arange(SLOTS, dtype=jnp.int32) == last_live).astype(jnp.float32)
    doc_sums = slot_sums[:SLOTS] + tail_pick[:, None] * carried_sum[None, :]
    total_tokens = tok_rows * seq_size
    later_starts = live_slot[None, :] & (doc_starts[None, :] > my_starts[:, None])
    following = jnp.min(jnp.where(later_starts, doc_starts[None, :], total_tokens), axis=1)
    doc_length = jnp.maximum(following - my_starts, 1).astype(jnp.float32)
    pooled = jnp.where(my_live[:, None], doc_sums / doc_length[:, None], 0.0)
    return (hidden, pooled)


def solution(mesh):
    grid = chip_grid(mesh)
    placed = (
        P(("groups", "seq"), None),
        P(("groups", "seq"), None),
        P(("groups", "seq"), None),
        P(("groups", "seq"), None),
        P("seq", None),
        P(),
        P("groups"),
    )

    def whole(*args):
        return body(grid, *args)

    step = jax.shard_map(
        whole,
        mesh=mesh,
        in_specs=placed,
        out_specs=(P(("groups", "seq"), None), P(("groups", "seq"), None)),
        check_vma=False,
    )

    def run(queries, keys, values, residual, out_weight, post_scale, doc_starts):
        args = (queries, keys, values, residual, out_weight, post_scale, doc_starts)
        return step(*args)

    return run
```

```python
import math

import jax
import jax.numpy as jnp
from jax import lax
from jax.experimental import pallas as pl
from jax.experimental.pallas import tpu as pltpu
from jax.sharding import PartitionSpec as P


HEAD_FEATURES = 128
WINDOW_SPAN = 1024
SLOTS = 2
LANES = 128
UNUSED = 2**30

query_scale = 168.0 ** (-0.5)
norm_eps = 1e-06


def chip_grid(mesh):
    devices = mesh.devices.reshape(mesh.shape["groups"], mesh.shape["seq"])
    where = [(*d.coords, d.core_on_chip) for d in devices[0]]
    xs = len({w[0] for w in where})
    zs = len({w[2] for w in where})
    if xs * zs * 2 != len(where):
        return None
    return zs, xs


def passed_along(block, axis, distance):
    devices = range(lax.axis_size(axis))
    route = [(i - distance, i) for i in devices if i - distance in devices]
    return lax.ppermute(block, axis, route)


def moved(block, grid, step):
    zs, xs = grid
    route = []
    for z in range(zs):
        for x in range(xs):
            for c in range(2):
                to = step(z, x, c)
                if to is not None:
                    route.append(((z * xs + x) * 2 + c, (to[0] * xs + to[1]) * 2 + to[2]))
    return lax.ppermute(block, "seq", route)


def last_start_at(pos, prev, s0, s1):
    last = jnp.maximum(prev, jnp.where(s0 <= pos, s0, 0))
    return jnp.maximum(last, jnp.where(s1 <= pos, s1, 0))


def attend(meta, queries, key_blocks, value_blocks, block_at, lower, upper, per_step):
    rows, width = queries.shape
    kv_width = key_blocks[0].shape[1]
    each = width // kv_width
    count = len(key_blocks)
    tall = each * rows
    to_exp2 = query_scale * math.log2(math.e)
    steps, skip = (upper - lower) // per_step, lower // per_step

    def kernel(meta, q_ref, *refs):
        k_refs, v_refs = refs[:count], refs[count : 2 * count]
        out_ref, bias, s_ref, m_ref, l_ref, acc = refs[2 * count :]
        first = meta[0] * rows
        prev, s0, s1 = meta[1], meta[2], meta[3]
        lowest = jnp.maximum(last_start_at(first, prev, s0, s1), first - WINDOW_SPAN + 1)
        places = []
        for b in range(count):
            index, valid = block_at(b, meta[0])
            start = index * rows
            places.append((start, valid & (index >= 0) & (start + rows > lowest)))

        @pl.when(pl.program_id(0) == 0)
        def _():
            for b, (start, need) in enumerate(places):

                @pl.when(need)
                def _():
                    q_pos = first + lax.broadcasted_iota(jnp.int32, (rows, rows), 0)
                    k_pos = start + lax.broadcasted_iota(jnp.int32, (rows, rows), 1)
                    low = last_start_at(q_pos, prev, s0, s1)
                    low = jnp.maximum(low, q_pos - WINDOW_SPAN + 1)
                    visible = (k_pos >= low) & (k_pos <= q_pos)
                    bias[b] = jnp.where(visible, 0.0, -jnp.inf)

        m_ref[...] = jnp.full(m_ref.shape, -jnp.inf, jnp.float32)
        l_ref[...] = jnp.zeros(l_ref.shape, jnp.float32)
        acc[...] = jnp.zeros(acc.shape, jnp.float32)

        def lanes(block):
            return [block[:, t : t + LANES] for t in range(0, rows, LANES)]

        for b, (start, need) in enumerate(places):

            @pl.when(need)
            def _():
                for g in range(per_step):
                    k = k_refs[b][:, g * HEAD_FEATURES : (g + 1) * HEAD_FEATURES]
                    for r in range(each):
                        at = (g * each + r) * HEAD_FEATURES
                        s = lax.dot_general(
                            q_ref[:, at : at + HEAD_FEATURES],
                            k,
                            (((1,), (1,)), ((), ())),
                            preferred_element_type=jnp.float32,
                        )
                        s = s + bias[b]
                        s_ref[b, g, r * rows : (r + 1) * rows] = s
                        top = m_ref[g, r * rows : (r + 1) * rows]
                        for part in lanes(s):
                            top = jnp.maximum(top, part)
                        m_ref[g, r * rows : (r + 1) * rows] = top

        for g in range(per_step):
            peak = jnp.max(m_ref[g], axis=1, keepdims=True)
            m_ref[g] = jnp.broadcast_to(peak, (tall, LANES))

        for b, (start, need) in enumerate(places):

            @pl.when(need)
            def _():
                for g in range(per_step):
                    peak = m_ref[g]
                    parts = [jnp.exp2((part - peak) * to_exp2) for part in lanes(s_ref[b, g])]
                    l_ref[g] += sum(parts[1:], parts[0])
                    p = jnp.concatenate([part.astype(jnp.bfloat16) for part in parts], axis=1)
                    acc[g] += jnp.dot(
                        p,
                        v_refs[b][:, g * HEAD_FEATURES : (g + 1) * HEAD_FEATURES],
                        preferred_element_type=jnp.float32,
                    )

        for g in range(per_step):
            totals = jnp.sum(l_ref[g], axis=1, keepdims=True)
            result = (acc[g] / totals).astype(jnp.bfloat16)
            for r in range(each):
                at = (g * each + r) * HEAD_FEATURES
                out_ref[:, at : at + HEAD_FEATURES] = result[r * rows : (r + 1) * rows]

    wide = per_step * each * HEAD_FEATURES
    q_spec = pl.BlockSpec((rows, wide), lambda g, meta: (0, g + skip))
    kv_spec = pl.BlockSpec((rows, per_step * HEAD_FEATURES), lambda g, meta: (0, g + skip))
    out_spec = pl.BlockSpec((rows, wide), lambda g, meta: (0, g))
    return pl.pallas_call(
        kernel,
        grid_spec=pltpu.PrefetchScalarGridSpec(
            num_scalar_prefetch=1,
            grid=(steps,),
            in_specs=[q_spec] + [kv_spec] * (2 * count),
            out_specs=out_spec,
            scratch_shapes=[
                pltpu.VMEM((count, rows, rows), jnp.float32),
                pltpu.VMEM((count, per_step, tall, rows), jnp.float32),
                pltpu.VMEM((per_step, tall, LANES), jnp.float32),
                pltpu.VMEM((per_step, tall, LANES), jnp.float32),
                pltpu.VMEM((per_step, tall, HEAD_FEATURES), jnp.float32),
            ],
        ),
        out_shape=jax.ShapeDtypeStruct((rows, steps * wide), jnp.bfloat16),
        name="attend",
    )(meta, queries, *key_blocks, *value_blocks)


def gathered(refs, w_ref, offs, sems):
    copies = []
    for i, ref in enumerate(refs):
        tall = ref.shape[0]
        at = pl.multiple_of(offs[i], math.gcd(tall, 16))
        copies.append(pltpu.make_async_copy(ref, w_ref.at[pl.ds(at, tall)], sems.at[i]))
    return copies


def joined(parts, whole_ref):
    at = 0
    for ref in parts:
        whole_ref[:, at : at + ref.shape[1]] = ref[...]
        at += ref.shape[1]


def column_spans(columns):
    return [(at, min(512, columns - at)) for at in range(0, columns, 512)]


def project(meta, chunk_at, attended, residual, post_scale, pieces, offsets, slots, seq_size):
    rows = attended[0].shape[0]
    width = sum(a.shape[1] for a in attended)
    columns = residual.shape[1]
    count = len(pieces)
    chunks = chunk_at.shape[0]
    chunk = width // chunks
    spans = column_spans(columns)
    lines = -(-columns // (8 * LANES)) * 8

    def kernel(meta, chunk_at, offs, post_ref, *refs):
        att_parts, refs = refs[: len(attended)], refs[len(attended) :]
        piece_refs, res_hbm = refs[:count], refs[count]
        hidden_ref, sums_ref, send_ref, w_ref, proj, att_ref, res_ref, row_ref, sems, res_sem = refs[
            count + 1 :
        ]
        copies = gathered(piece_refs, w_ref, offs, sems)
        for i in range(chunks):
            for copy, slot in zip(copies, slots):
                if slot == i:
                    copy.start()
        res_copy = pltpu.make_async_copy(res_hbm, res_ref, res_sem)
        res_copy.start()
        joined(att_parts, att_ref)
        first = meta[0] * rows
        prev, s0, s1 = meta[1], meta[2], meta[3]
        pos = first + lax.broadcasted_iota(jnp.int32, (rows, LANES), 0)
        last = last_start_at(pos, prev, s0, s1)
        masks = [m.astype(jnp.float32) for m in (last == s0, last == s1, last < first)]
        square = jnp.zeros((rows, LANES), jnp.float32)
        for i in range(chunks):
            for copy, slot in zip(copies, slots):
                if slot == i:
                    copy.wait()
            att = att_ref[:, pl.ds(pl.multiple_of(chunk_at[i] * chunk, LANES), chunk)]
            for at, split in spans:
                part = jnp.dot(
                    att,
                    w_ref[i * chunk : (i + 1) * chunk, at : at + split],
                    preferred_element_type=jnp.float32,
                )
                if i > 0:
                    part = part + proj[:, at : at + split]
                proj[:, at : at + split] = part
                if i == chunks - 1:
                    for t in range(0, split, LANES):
                        square = square + part[:, t : t + LANES] * part[:, t : t + LANES]
        total = jnp.sum(square, axis=1, keepdims=True)
        norm = jnp.broadcast_to(lax.rsqrt(total * (1.0 / columns) + norm_eps), (rows, LANES))
        owner = prev // rows
        res_copy.wait()
        send_ref[...] = jnp.zeros(send_ref.shape, send_ref.dtype)
        row_ref[...] = jnp.zeros(row_ref.shape, jnp.float32)
        for at in range(0, columns, LANES):
            updated = res_ref[:, at : at + LANES].astype(jnp.float32) + (
                proj[:, at : at + LANES] * norm * post_ref[:, at : at + LANES]
            )
            hidden_ref[:, at : at + LANES] = updated.astype(jnp.bfloat16)
            sums = [jnp.sum(updated * m, axis=0, keepdims=True) for m in masks]
            for slot in range(SLOTS):
                sums_ref[slot : slot + 1, at : at + LANES] = sums[slot]
            row_ref[at // LANES : at // LANES + 1, :] = sums[SLOTS]
        send_ref[owner] = row_ref[...].astype(send_ref.dtype)

    whole = pl.BlockSpec(memory_space=pltpu.MemorySpace.VMEM)
    smem = pl.BlockSpec(memory_space=pltpu.MemorySpace.SMEM)
    return pl.pallas_call(
        kernel,
        in_specs=[smem, smem, smem, whole]
        + [whole] * len(attended)
        + [pl.BlockSpec(memory_space=pl.ANY)] * (count + 1),
        out_specs=(whole, whole, whole),
        out_shape=(
            jax.ShapeDtypeStruct((rows, columns), jnp.bfloat16),
            jax.ShapeDtypeStruct((SLOTS, columns), jnp.float32),
            jax.ShapeDtypeStruct((seq_size, lines, LANES), jnp.bfloat16),
        ),
        scratch_shapes=[
            pltpu.VMEM((width, columns), jnp.bfloat16),
            pltpu.VMEM((rows, columns), jnp.float32),
            pltpu.VMEM((rows, width), jnp.bfloat16),
            pltpu.VMEM((rows, columns), jnp.bfloat16),
            pltpu.VMEM((lines, LANES), jnp.float32),
            pltpu.SemaphoreType.DMA((count,)),
            pltpu.SemaphoreType.DMA,
        ],
        name="project",
    )(meta, chunk_at, offsets, post_scale[None, :], *attended, *pieces, residual)


def by_links(grid, groups, tok_rows, part_rows):
    return grid == (4, 2) and groups == 2 and WINDOW_SPAN == 4 * tok_rows and part_rows % 32 == 0


def body(grid, queries, keys, values, residual, out_weight, post_scale, doc_starts):
    seq_size = lax.axis_size("seq")
    my_index = lax.axis_index("seq")
    tok_rows = queries.shape[0]
    halo_blocks = WINDOW_SPAN // tok_rows
    part_rows = out_weight.shape[0]
    kv_heads = keys.shape[1] // HEAD_FEATURES

    slot_count = doc_starts.shape[0]
    slot_ids = jnp.arange(slot_count, dtype=jnp.int32)
    live_slot = doc_starts < (slot_ids // SLOTS + 1) * tok_rows
    first = my_index * tok_rows
    my_starts = lax.dynamic_slice_in_dim(doc_starts, my_index * SLOTS, SLOTS)
    my_live = my_starts < first + tok_rows
    prev = jnp.max(jnp.where(live_slot & (doc_starts < first), doc_starts, 0))
    shown = jnp.where(my_live, my_starts, UNUSED)
    meta = jnp.concatenate([my_index[None], prev[None], shown]).astype(jnp.int32)

    if by_links(grid, lax.axis_size("groups"), tok_rows, part_rows):
        zs, xs = grid
        half_rows = part_rows // 2
        z, x, c = my_index // 4, my_index // 2 % 2, my_index % 2
        y = lax.axis_index("groups")

        def turned(k):
            return lambda block: moved(block, grid, lambda z, x, c: ((z + k) % zs, x, c))

        def over_x(block):
            return moved(block, grid, lambda z, x, c: (z, 1 - x, c))

        def over_c(block):
            return moved(block, grid, lambda z, x, c: (z, x, 1 - c))

        def over_y(block):
            return lax.ppermute(block, "groups", [(0, 1), (1, 0)])

        def up(block):
            return moved(block, grid, lambda z, x, c: (z + 1, x, c) if z + 1 < zs else None)

        def right(block):
            return moved(block, grid, lambda z, x, c: (z, x, 1) if c == 0 else None)

        def left(block):
            return moved(block, grid, lambda z, x, c: (z, x, 0) if c == 1 else None)

        own = lax.dynamic_slice_in_dim(out_weight, y * half_rows, half_rows)
        pieces, offsets, slots = [], [], []

        def place(slot, piece, x, c, half):
            pieces.append(piece)
            offsets.append((slot * xs * 2 + x * 2 + c) * part_rows + half * half_rows)
            slots.append(slot)

        def place_all(slot, piece, x):
            other = over_y(piece)
            place(slot, piece, x, c, y)
            place(slot, other, x, c, 1 - y)
            place(slot, over_c(piece), x, 1 - c, y)
            place(slot, over_c(other), x, 1 - c, 1 - y)

        place(0, out_weight, x, c, 0)
        place(0, over_c(out_weight), x, 1 - c, 0)
        place_all(0, over_x(own), 1 - x)
        nearest = turned(1)(own)
        for slot, k in ((1, 1), (2, 3), (3, 2)):
            ring = nearest
            if k == 2:
                ring = turned(1)(nearest)
            if k == 3:
                ring = turned(3)(own)
            place_all(slot, ring, x)
            place_all(slot, over_x(ring), 1 - x)
        chunk_at = jnp.stack([z, (z - 1) % zs, (z - 3) % zs, (z - 2) % zs]).astype(jnp.int32)
        offsets = jnp.stack([jnp.asarray(o, jnp.int32) for o in offsets])

        groups = []
        for mine in (keys, values):
            below = up(mine)
            onward = jnp.where(x == 0, mine, below)
            aside = over_x(onward)
            groups.append([mine, right(mine), below, left(below), aside, over_c(aside)])
        key_blocks, value_blocks = groups

        def block_at(b, index):
            chip, core = index // 2, index % 2
            back = (0, 0, 2, 2, 1, 1)[b]
            place = (chip - back) * 2 + (core if b % 2 == 0 else 1 - core)
            valid = True
            if b == 1:
                valid = core == 1
            if b == 3:
                valid = core == 0
            return place, (place <= index) & valid

        attended = []
        half = kv_heads // 2
        for lower in (0, half):
            attended.append(
                attend(meta, queries, key_blocks, value_blocks, block_at, lower, lower + half, half)
            )
    else:
        pieces = [lax.all_gather(out_weight, "seq", axis=0, tiled=True)]
        offsets = jnp.zeros((1,), jnp.int32)
        chunk_at, slots = offsets, [0]
        key_blocks, value_blocks = [keys], [values]
        for distance in range(1, halo_blocks + 1):
            key_blocks.append(passed_along(keys, "seq", distance))
            value_blocks.append(passed_along(values, "seq", distance))

        def block_at(b, index):
            return index - b, index >= b

        attended = [
            attend(
                meta, queries, key_blocks, value_blocks, block_at, 0, kv_heads, math.gcd(kv_heads, 4)
            )
        ]

    hidden, slot_sums, send = project(
        meta, chunk_at, attended, residual, post_scale, pieces, offsets, slots, seq_size
    )
    arrived = lax.all_to_all(send, "seq", 0, 0, tiled=True)
    carried_sum = jnp.sum(arrived.astype(jnp.float32), axis=0).reshape(-1)[: residual.shape[1]]
    last_live = jnp.sum(my_live.astype(jnp.int32)) - 1
    tail_pick = (jnp.arange(SLOTS, dtype=jnp.int32) == last_live).astype(jnp.float32)
    doc_sums = slot_sums + tail_pick[:, None] * carried_sum[None, :]
    total_tokens = tok_rows * seq_size
    later_starts = live_slot[None, :] & (doc_starts[None, :] > my_starts[:, None])
    following = jnp.min(jnp.where(later_starts, doc_starts[None, :], total_tokens), axis=1)
    doc_length = jnp.maximum(following - my_starts, 1).astype(jnp.float32)
    pooled = jnp.where(my_live[:, None], doc_sums / doc_length[:, None], 0.0)
    return (hidden, pooled)


def solution(mesh):
    grid = chip_grid(mesh)
    placed = (
        P(("groups", "seq"), None),
        P(("groups", "seq"), None),
        P(("groups", "seq"), None),
        P(("groups", "seq"), None),
        P("seq", None),
        P(),
        P("groups"),
    )

    def whole(*args):
        return body(grid, *args)

    step = jax.shard_map(
        whole,
        mesh=mesh,
        in_specs=placed,
        out_specs=(P(("groups", "seq"), None), P(("groups", "seq"), None)),
        check_vma=False,
    )

    def run(queries, keys, values, residual, out_weight, post_scale, doc_starts):
        args = (queries, keys, values, residual, out_weight, post_scale, doc_starts)
        return step(*args)

    return run
```

```python
import math

import jax
import jax.numpy as jnp
from jax import lax
from jax.experimental import pallas as pl
from jax.experimental.pallas import tpu as pltpu
from jax.sharding import PartitionSpec as P


HEAD_FEATURES = 128
WINDOW_SPAN = 1024
SLOTS = 2
LANES = 128
UNUSED = 2**30

query_scale = 168.0 ** (-0.5)
norm_eps = 1e-06


def chip_grid(mesh):
    devices = mesh.devices.reshape(mesh.shape["groups"], mesh.shape["seq"])
    where = [(*d.coords, d.core_on_chip) for d in devices[0]]
    xs = len({w[0] for w in where})
    zs = len({w[2] for w in where})
    if xs * zs * 2 != len(where):
        return None
    return zs, xs


def passed_along(block, axis, distance):
    devices = range(lax.axis_size(axis))
    route = [(i - distance, i) for i in devices if i - distance in devices]
    return lax.ppermute(block, axis, route)


def moved(block, grid, step):
    zs, xs = grid
    route = []
    for z in range(zs):
        for x in range(xs):
            for c in range(2):
                to = step(z, x, c)
                if to is not None:
                    route.append(((z * xs + x) * 2 + c, (to[0] * xs + to[1]) * 2 + to[2]))
    return lax.ppermute(block, "seq", route)


def last_start_at(pos, prev, s0, s1):
    last = jnp.maximum(prev, jnp.where(s0 <= pos, s0, 0))
    return jnp.maximum(last, jnp.where(s1 <= pos, s1, 0))


def my_docs(starts_ref, my_index, rows):
    def one(device, prev):
        end = (device + 1) * rows
        for t in range(SLOTS):
            start = starts_ref[device * SLOTS + t]
            prev = jnp.maximum(prev, jnp.where(start < end, start, 0))
        return prev

    prev = lax.fori_loop(0, my_index, one, 0)
    end = (my_index + 1) * rows
    mine = [starts_ref[my_index * SLOTS + t] for t in range(SLOTS)]
    return [prev] + [jnp.where(start < end, start, UNUSED) for start in mine]


def attend(index, doc_starts, queries, key_blocks, value_blocks, block_at, lower, upper):
    rows, width = queries.shape
    kv_width = key_blocks[0].shape[1]
    each = width // kv_width
    count = len(key_blocks)
    tall = each * rows
    to_exp2 = query_scale * math.log2(math.e)
    heads = upper - lower
    narrow = heads * HEAD_FEATURES
    wide = each * narrow

    def kernel(index_ref, starts_ref, q_hbm, *refs):
        k_hbms, v_hbms = refs[:count], refs[count : 2 * count]
        out_ref, bias, s_ref, m_ref, l_ref, acc, q_ref, k_ref, v_ref, sems = refs[2 * count :]
        my_index = index_ref[0]
        first = my_index * rows
        prev, s0, s1 = my_docs(starts_ref, my_index, rows)
        lowest = jnp.maximum(last_start_at(first, prev, s0, s1), first - WINDOW_SPAN + 1)
        places = []
        for b in range(count):
            at, valid = block_at(b, my_index)
            start = at * rows
            places.append((start, valid & (at >= 0) & (start + rows > lowest)))

        q_copy = pltpu.make_async_copy(
            q_hbm.at[:, lower * each * HEAD_FEATURES : upper * each * HEAD_FEATURES],
            q_ref,
            sems.at[2 * count],
        )
        kv_copies = [
            pltpu.make_async_copy(
                ref.at[:, lower * HEAD_FEATURES : upper * HEAD_FEATURES],
                buffer.at[b],
                sems.at[b + at],
            )
            for at, buffer, hbms in ((0, k_ref, k_hbms), (count, v_ref, v_hbms))
            for b, ref in enumerate(hbms)
        ]
        q_copy.start()
        for copies in (kv_copies[:count], kv_copies[count:]):
            for copy, (start, need) in zip(copies, places):
                pl.when(need)(copy.start)

        for b, (start, need) in enumerate(places):

            @pl.when(need)
            def _():
                q_pos = first + lax.broadcasted_iota(jnp.int32, (rows, rows), 0)
                k_pos = start + lax.broadcasted_iota(jnp.int32, (rows, rows), 1)
                low = last_start_at(q_pos, prev, s0, s1)
                low = jnp.maximum(low, q_pos - WINDOW_SPAN + 1)
                visible = (k_pos >= low) & (k_pos <= q_pos)
                bias[b] = jnp.where(visible, 0.0, -jnp.inf)

        m_ref[...] = jnp.full(m_ref.shape, -jnp.inf, jnp.float32)
        l_ref[...] = jnp.zeros(l_ref.shape, jnp.float32)
        acc[...] = jnp.zeros(acc.shape, jnp.float32)

        def lanes(block):
            return [block[:, t : t + LANES] for t in range(0, rows, LANES)]

        q_copy.wait()
        for b, (start, need) in enumerate(places):

            @pl.when(need)
            def _():
                kv_copies[b].wait()
                for g in range(heads):
                    k = k_ref[b, :, g * HEAD_FEATURES : (g + 1) * HEAD_FEATURES]
                    for r in range(each):
                        at = (g * each + r) * HEAD_FEATURES
                        s = lax.dot_general(
                            q_ref[:, at : at + HEAD_FEATURES],
                            k,
                            (((1,), (1,)), ((), ())),
                            preferred_element_type=jnp.float32,
                        )
                        s = s + bias[b]
                        s_ref[b, g, r * rows : (r + 1) * rows] = s
                        top = m_ref[g, r * rows : (r + 1) * rows]
                        for part in lanes(s):
                            top = jnp.maximum(top, part)
                        m_ref[g, r * rows : (r + 1) * rows] = top

        for g in range(heads):
            peak = jnp.max(m_ref[g], axis=1, keepdims=True)
            m_ref[g] = jnp.broadcast_to(peak, (tall, LANES))

        for b, (start, need) in enumerate(places):

            @pl.when(need)
            def _():
                kv_copies[count + b].wait()
                for g in range(heads):
                    peak = m_ref[g]
                    parts = [jnp.exp2((part - peak) * to_exp2) for part in lanes(s_ref[b, g])]
                    l_ref[g] += sum(parts[1:], parts[0])
                    p = jnp.concatenate([part.astype(jnp.bfloat16) for part in parts], axis=1)
                    acc[g] += jnp.dot(
                        p,
                        v_ref[b, :, g * HEAD_FEATURES : (g + 1) * HEAD_FEATURES],
                        preferred_element_type=jnp.float32,
                    )

        for g in range(heads):
            totals = jnp.sum(l_ref[g], axis=1, keepdims=True)
            result = (acc[g] / totals).astype(jnp.bfloat16)
            for r in range(each):
                at = (g * each + r) * HEAD_FEATURES
                out_ref[:, at : at + HEAD_FEATURES] = result[r * rows : (r + 1) * rows]

    smem = pl.BlockSpec(memory_space=pltpu.MemorySpace.SMEM)
    return pl.pallas_call(
        kernel,
        in_specs=[smem, smem] + [pl.BlockSpec(memory_space=pl.ANY)] * (2 * count + 1),
        out_specs=pl.BlockSpec(memory_space=pltpu.MemorySpace.VMEM),
        scratch_shapes=[
            pltpu.VMEM((count, rows, rows), jnp.float32),
            pltpu.VMEM((count, heads, tall, rows), jnp.float32),
            pltpu.VMEM((heads, tall, LANES), jnp.float32),
            pltpu.VMEM((heads, tall, LANES), jnp.float32),
            pltpu.VMEM((heads, tall, HEAD_FEATURES), jnp.float32),
            pltpu.VMEM((rows, wide), jnp.bfloat16),
            pltpu.VMEM((count, rows, narrow), jnp.bfloat16),
            pltpu.VMEM((count, rows, narrow), jnp.bfloat16),
            pltpu.SemaphoreType.DMA((2 * count + 1,)),
        ],
        out_shape=jax.ShapeDtypeStruct((rows, wide), jnp.bfloat16),
        name="attend",
    )(index, doc_starts, queries, *key_blocks, *value_blocks)


def joined(parts, whole_ref):
    at = 0
    for ref in parts:
        whole_ref[:, at : at + ref.shape[1]] = ref[...]
        at += ref.shape[1]


def column_spans(columns):
    return [(at, min(512, columns - at)) for at in range(0, columns, 512)]


def project(index, group, doc_starts, attended, residual, post, pieces, row_at, chunk_of, slots):
    rows = attended[0].shape[0]
    width = sum(a.shape[1] for a in attended)
    columns = residual.shape[1]
    count = len(pieces)
    parts = len(attended)
    chunks = max(slots) + 1
    chunk = width // chunks
    spans = column_spans(columns)
    lines = -(-columns // (8 * LANES)) * 8
    slot_count = doc_starts.shape[0]
    seq_size = slot_count // SLOTS

    def kernel(index_ref, group_ref, starts_ref, post_ref, *refs):
        att_parts, piece_refs, res_hbm = refs[:parts], refs[parts : parts + count], refs[parts + count]
        hidden_ref, base_ref, share_ref, send_ref = refs[parts + count + 1 : parts + count + 5]
        w_ref, proj, att_ref, res_ref, row_ref, sems, res_sem = refs[parts + count + 5 :]
        my_index = index_ref[0]
        group = group_ref[0]
        spot = (my_index >> 2, (my_index >> 1) & 1, my_index & 1)
        copies = []
        for i, ref in enumerate(piece_refs):
            tall = ref.shape[0]
            at = slots[i] * chunk + row_at(i, spot, group)
            at = pl.multiple_of(at, math.gcd(tall, 16))
            copies.append(pltpu.make_async_copy(ref, w_ref.at[pl.ds(at, tall)], sems.at[i]))
        res_copy = pltpu.make_async_copy(res_hbm, res_ref, res_sem)
        for i in range(chunks):
            for copy, slot in zip(copies, slots):
                if slot == i:
                    copy.start()
        res_copy.start()
        joined(att_parts, att_ref)

        first = my_index * rows
        prev, s0, s1 = my_docs(starts_ref, my_index, rows)

        def next_start(device, least):
            end = (device + 1) * rows
            for t in range(SLOTS):
                start = starts_ref[device * SLOTS + t]
                least = jnp.minimum(least, jnp.where(start < end, start, seq_size * rows))
            return least

        beyond = lax.fori_loop(my_index + 1, seq_size, next_start, seq_size * rows)
        lengths = (jnp.minimum(s1, beyond) - s0, beyond - s1)
        lengths = [
            jnp.full((1, LANES), jnp.maximum(length, 1), jnp.int32).astype(jnp.float32)
            for length in lengths
        ]
        tails = ((s0 < UNUSED) & (s1 == UNUSED), s1 < UNUSED)
        for slot in range(SLOTS):
            tail = jnp.full((1, LANES), tails[slot].astype(jnp.int32)).astype(jnp.float32)
            share_ref[slot : slot + 1, :] = tail / lengths[slot]
        pos = first + lax.broadcasted_iota(jnp.int32, (rows, LANES), 0)
        last = last_start_at(pos, prev, s0, s1)
        masks = [m.astype(jnp.float32) for m in (last == s0, last == s1, last < first)]
        send_ref[...] = jnp.zeros(send_ref.shape, send_ref.dtype)
        row_ref[...] = jnp.zeros(row_ref.shape, jnp.float32)

        square = jnp.zeros((rows, LANES), jnp.float32)
        for i in range(chunks):
            for copy, slot in zip(copies, slots):
                if slot == i:
                    copy.wait()
            from_column = pl.multiple_of(chunk_of(i, spot) * chunk, LANES)
            att = att_ref[:, pl.ds(from_column, chunk)]
            for at, split in spans:
                part = jnp.dot(
                    att,
                    w_ref[i * chunk : (i + 1) * chunk, at : at + split],
                    preferred_element_type=jnp.float32,
                )
                if i > 0:
                    part = part + proj[:, at : at + split]
                proj[:, at : at + split] = part
                if i == chunks - 1:
                    for t in range(0, split, LANES):
                        square = square + part[:, t : t + LANES] * part[:, t : t + LANES]
        total = jnp.sum(square, axis=1, keepdims=True)
        norm = jnp.broadcast_to(lax.rsqrt(total * (1.0 / columns) + norm_eps), (rows, LANES))
        res_copy.wait()
        for at in range(0, columns, LANES):
            updated = res_ref[:, at : at + LANES].astype(jnp.float32) + (
                proj[:, at : at + LANES] * norm * post_ref[:, at : at + LANES]
            )
            hidden_ref[:, at : at + LANES] = updated.astype(jnp.bfloat16)
            sums = [jnp.sum(updated * m, axis=0, keepdims=True) for m in masks]
            for slot in range(SLOTS):
                base_ref[slot : slot + 1, at : at + LANES] = sums[slot]
            row_ref[at // LANES : at // LANES + 1, :] = sums[SLOTS]
        send_ref[lax.div(prev, rows)] = row_ref[...].astype(send_ref.dtype)
        inverse = jnp.concatenate([1.0 / length for length in lengths], axis=0)
        for at in range(0, columns, LANES):
            base_ref[:, at : at + LANES] = base_ref[:, at : at + LANES] * inverse

    whole = pl.BlockSpec(memory_space=pltpu.MemorySpace.VMEM)
    smem = pl.BlockSpec(memory_space=pltpu.MemorySpace.SMEM)
    return pl.pallas_call(
        kernel,
        in_specs=[smem, smem, smem]
        + [whole] * (parts + 1)
        + [pl.BlockSpec(memory_space=pl.ANY)] * (count + 1),
        out_specs=(whole, whole, whole, whole),
        out_shape=(
            jax.ShapeDtypeStruct((rows, columns), jnp.bfloat16),
            jax.ShapeDtypeStruct((SLOTS, columns), jnp.float32),
            jax.ShapeDtypeStruct((SLOTS, LANES), jnp.float32),
            jax.ShapeDtypeStruct((seq_size, lines, LANES), jnp.bfloat16),
        ),
        scratch_shapes=[
            pltpu.VMEM((width, columns), jnp.bfloat16),
            pltpu.VMEM((rows, columns), jnp.float32),
            pltpu.VMEM((rows, width), jnp.bfloat16),
            pltpu.VMEM((rows, columns), jnp.bfloat16),
            pltpu.VMEM((lines, LANES), jnp.float32),
            pltpu.SemaphoreType.DMA((count,)),
            pltpu.SemaphoreType.DMA,
        ],
        name="project",
    )(index, group, doc_starts, post, *attended, *pieces, residual)


def by_links(grid, groups, tok_rows, part_rows):
    return grid == (4, 2) and groups == 2 and WINDOW_SPAN == 4 * tok_rows and part_rows % 32 == 0


def body(grid, queries, keys, values, residual, out_weight, post_scale, doc_starts):
    my_index = lax.axis_index("seq")
    tok_rows = queries.shape[0]
    halo_blocks = WINDOW_SPAN // tok_rows
    part_rows = out_weight.shape[0]
    kv_heads = keys.shape[1] // HEAD_FEATURES

    index = my_index.reshape(1).astype(jnp.int32)
    group = lax.axis_index("groups").reshape(1).astype(jnp.int32)
    post = post_scale[None, :]

    if by_links(grid, lax.axis_size("groups"), tok_rows, part_rows):
        zs, _ = grid
        half_rows = part_rows // 2
        x = my_index // 2 % 2
        y = lax.axis_index("groups")

        def turned(k):
            return lambda block: moved(block, grid, lambda z, x, c: ((z + k) % zs, x, c))

        def over_x(block):
            return moved(block, grid, lambda z, x, c: (z, 1 - x, c))

        def over_c(block):
            return moved(block, grid, lambda z, x, c: (z, x, 1 - c))

        def over_y(block):
            return lax.ppermute(block, "groups", [(0, 1), (1, 0)])

        def up(block):
            return moved(block, grid, lambda z, x, c: (z + 1, x, c) if z + 1 < zs else None)

        def right(block):
            return moved(block, grid, lambda z, x, c: (z, x, 1) if c == 0 else None)

        def left(block):
            return moved(block, grid, lambda z, x, c: (z, x, 0) if c == 1 else None)

        own = lax.dynamic_slice_in_dim(out_weight, y * half_rows, half_rows)
        pieces, slots, sides = [], [], []

        def place(slot, piece, over_x, over_c, half):
            pieces.append(piece)
            slots.append(slot)
            sides.append((over_x, over_c, half))

        def place_all(slot, piece, side):
            other = over_y(piece)
            place(slot, piece, side, 0, "mine")
            place(slot, other, side, 0, "other")
            place(slot, over_c(piece), side, 1, "mine")
            place(slot, over_c(other), side, 1, "other")

        place(0, out_weight, 0, 0, "both")
        place(0, over_c(out_weight), 0, 1, "both")
        place_all(0, over_x(own), 1)
        nearest = turned(1)(own)
        for slot, k in ((1, 1), (2, 3), (3, 2)):
            ring = nearest
            if k == 2:
                ring = turned(1)(nearest)
            if k == 3:
                ring = turned(3)(own)
            place_all(slot, ring, 0)
            place_all(slot, over_x(ring), 1)

        def row_at(i, spot, group):
            side_x, side_c, half = sides[i]
            _, x, c = spot
            x, c = (1 - x if side_x else x), (1 - c if side_c else c)
            half = {"both": 0, "mine": group, "other": 1 - group}[half]
            return (x * 2 + c) * part_rows + half * half_rows

        def chunk_of(slot, spot):
            return (spot[0] + zs - (0, 1, 3, 2)[slot]) & (zs - 1)

        groups = []
        for mine in (keys, values):
            below = up(mine)
            onward = jnp.where(x == 0, mine, below)
            aside = over_x(onward)
            groups.append([mine, right(mine), below, left(below), aside, over_c(aside)])
        key_blocks, value_blocks = groups

        def block_at(b, index):
            chip, core = index >> 1, index & 1
            back = (0, 0, 2, 2, 1, 1)[b]
            place = (chip - back) * 2 + (core if b % 2 == 0 else 1 - core)
            valid = True
            if b == 1:
                valid = core == 1
            if b == 3:
                valid = core == 0
            return place, (place <= index) & valid

        attended = []
        half = kv_heads // 2
        for lower in (0, half):
            attended.append(
                attend(
                    index,
                    doc_starts,
                    queries,
                    key_blocks,
                    value_blocks,
                    block_at,
                    lower,
                    lower + half,
                )
            )
    else:
        pieces, slots = [lax.all_gather(out_weight, "seq", axis=0, tiled=True)], [0]
        key_blocks, value_blocks = [keys], [values]
        for distance in range(1, halo_blocks + 1):
            key_blocks.append(passed_along(keys, "seq", distance))
            value_blocks.append(passed_along(values, "seq", distance))

        def block_at(b, index):
            return index - b, index >= b

        def row_at(i, spot, group):
            return 0

        def chunk_of(slot, spot):
            return 0

        few = math.gcd(kv_heads, 4)
        attended = [
            attend(
                index, doc_starts, queries, key_blocks, value_blocks, block_at, lower, lower + few
            )
            for lower in range(0, kv_heads, few)
        ]

    hidden, base, share, send = project(
        index, group, doc_starts, attended, residual, post, pieces, row_at, chunk_of, slots
    )
    arrived = lax.all_to_all(send, "seq", 0, 0, tiled=True)
    carried_sum = jnp.sum(arrived.astype(jnp.float32), axis=0).reshape(-1)[: residual.shape[1]]
    pooled = base + share[:, :1] * carried_sum[None, :]
    return (hidden, pooled)


def solution(mesh):
    grid = chip_grid(mesh)
    placed = (
        P(("groups", "seq"), None),
        P(("groups", "seq"), None),
        P(("groups", "seq"), None),
        P(("groups", "seq"), None),
        P("seq", None),
        P(),
        P("groups"),
    )

    def whole(*args):
        return body(grid, *args)

    step = jax.shard_map(
        whole,
        mesh=mesh,
        in_specs=placed,
        out_specs=(P(("groups", "seq"), None), P(("groups", "seq"), None)),
        check_vma=False,
    )

    def run(queries, keys, values, residual, out_weight, post_scale, doc_starts):
        args = (queries, keys, values, residual, out_weight, post_scale, doc_starts)
        return step(*args)

    return run
```
